512 devices in a mesh: seq: 32 (over x, y, core), head: 16 (over z).
Axes of the slice: x: 4, y: 4, z: 16, core: 2. Of those that a mesh axis runs over, the one named last changes fastest.
Arguments:
- queries: bfloat16 [65536, 4096], P(('seq', 'head')), may hold values from -6 to 6
- keys: bfloat16 [65536, 4096], P(('seq', 'head')), may hold values from -6 to 6
- values: bfloat16 [65536, 4096], P(('seq', 'head')), may hold values from -60 to 60
- gain: float32 [4096], replicated, may hold values from 0.1 to 1.9
Outputs:
- normed: bfloat16 [65536, 4096], P(('seq', 'head'))
The draws below stay inside these ranges and needn't reach their ends.
All inputs are finite; a program needn't handle non-finite values.
Results may differ from the reference program's by a relative error of at most 0.015.
Values may be sent and summed in bfloat16 or wider, within the bound.
A program may use at most 64 MiB of HBM per device.

```python
import jax
import jax.numpy as jnp
from jax import lax

E = 128
HEADS = 32
TOKENS = 65536
FEAT = 4096
BLOCK = 128


def draw_values(key, part):
    first = jax.random.fold_in(key, 0)
    heads = jnp.arange(HEADS, dtype=jnp.float32)
    scales = 10.0 ** (heads / (HEADS - 1))
    base = jax.random.truncated_normal(first, -6.0, 6.0, (TOKENS, HEADS, E), jnp.float32)
    return (base * scales[None, :, None]).reshape(TOKENS, HEADS * E).astype(jnp.bfloat16)


def level_of(stream_key, shape, pieces, low, top_value):
    factor_of, own = 1.0, jax.random.fold_in(stream_key, 6)
    for axis_at, parts in pieces:
        heights = jnp.exp(jax.random.uniform(jax.random.fold_in(own, axis_at), (parts,), jnp.float32, low / len(pieces), top_value / len(pieces)))
        factor_of = factor_of * jnp.repeat(heights, shape[axis_at] // parts).reshape([-1 if axis == axis_at else 1 for axis in range(len(shape))])
    return factor_of


def centred(stream_key, extent, spread, most, cuts=(), kind=jnp.bfloat16):
    level = level_of(stream_key, extent, cuts, -0.22, 0.18) if cuts else 1.0
    values = jax.random.normal(stream_key, extent, jnp.float32) * spread * level
    return jnp.minimum(jnp.maximum(values, -most), most).astype(kind)


def setup_inputs(seed: int = 0) -> dict:
    key_list = jax.random.split(jax.random.key(seed), 5)
    return {
        "queries": centred(key_list[0], (TOKENS, FEAT), 1.0, 6.0, ((0, 512),)),
        "keys": centred(key_list[1], (TOKENS, FEAT), 1.0, 6.0, ((0, 512),)),
        "values": draw_values(jax.random.fold_in(key_list[4], 71), 0),
        "gain": jnp.clip(1.0 + 0.18 * jax.random.normal(key_list[3], (FEAT,), jnp.float32), 0.1, 1.9),
    }


def reference(queries, keys, values, gain):
    count = TOKENS // BLOCK
    qb = queries.reshape(count, BLOCK, HEADS, E)
    kb = keys.reshape(count, BLOCK, HEADS, E)
    vb = values.reshape(count, BLOCK, HEADS, E)
    lower = jnp.tril(jnp.ones((BLOCK, BLOCK), dtype=bool))

    def advance(state, blocks):
        qf = blocks[0].astype(jnp.float32)
        kf = blocks[1].astype(jnp.float32)
        vf = blocks[2].astype(jnp.float32)
        scores = jnp.einsum('thd,shd->hts', qf, kf)
        scores = jnp.where(lower[None], scores, 0.0).astype(jnp.bfloat16)
        scores = lax.optimization_barrier(scores).astype(jnp.float32)
        state_round = lax.optimization_barrier(state.astype(jnp.bfloat16)).astype(jnp.float32)
        inner = jnp.einsum('hts,shd->thd', scores, vf)
        outer = jnp.einsum('thd,hde->the', qf, state_round)
        attended = (inner + outer).astype(jnp.bfloat16)
        state = state + jnp.einsum('shd,she->hde', kf, vf)
        return (state, attended)
    start = jnp.zeros((HEADS, E, E), jnp.float32)
    last, attended = lax.scan(advance, start, (qb, kb, vb))
    attended = attended.reshape(TOKENS, FEAT).astype(jnp.float32)
    meansq = lax.optimization_barrier(jnp.mean(attended * attended, axis=1, keepdims=True))
    normed = attended * lax.rsqrt(meansq + 1e-06) * gain[None, :]
    return normed.astype(jnp.bfloat16)
```

```python
import jax
import jax.numpy as jnp
from jax import lax
from jax.sharding import PartitionSpec as P

E = 128
HEADS = 32


def per_device(queries, keys, values, gain):
    groups = lax.axis_size("head")
    local_heads = HEADS // groups
    block = queries.shape[0]
    zpos = lax.axis_index("head")
    gpos = lax.axis_index("seq")
    q = queries.reshape(block, HEADS, E)
    k = keys.reshape(block, HEADS, E)
    v = values.reshape(block, HEADS, E)
    own = jnp.einsum("shd,she->hde", k, v, preferred_element_type=jnp.float32)
    own = own.astype(jnp.bfloat16)
    states = lax.all_to_all(
        own.reshape(groups, local_heads, E, E), "head", split_axis=0, concat_axis=0, tiled=True
    ).astype(jnp.float32)
    total = jnp.sum(states, axis=0).astype(jnp.bfloat16)
    totals = lax.all_gather(total, "seq").astype(jnp.float32)
    count = totals.shape[0]
    reached = (jnp.arange(count) < gpos)[:, None, None, None]
    earlier = jnp.sum(jnp.where(reached, totals, 0.0), axis=0)
    entering = earlier[None] + jnp.cumsum(states, axis=0) - states
    entering = entering.astype(jnp.bfloat16)
    state = lax.all_to_all(entering, "head", split_axis=0, concat_axis=0, tiled=True)
    state = state.reshape(HEADS, E, E)
    lower = jnp.tril(jnp.ones((block, block), dtype=bool))
    scores = jnp.einsum("thd,shd->hts", q, k, preferred_element_type=jnp.float32)
    scores = jnp.where(lower[None], scores, 0.0).astype(jnp.bfloat16)
    inner = jnp.einsum("hts,shd->thd", scores, v, preferred_element_type=jnp.float32)
    outer = jnp.einsum("thd,hde->the", q, state, preferred_element_type=jnp.float32)
    home = (inner + outer).astype(jnp.bfloat16).reshape(block, HEADS * E).astype(jnp.float32)
    meansq = jnp.mean(home * home, axis=1, keepdims=True)
    return (home * lax.rsqrt(meansq + 1e-06) * gain[None, :]).astype(jnp.bfloat16)


def solution(mesh):
    return jax.shard_map(
        per_device,
        mesh=mesh,
        in_specs=(
            P(("seq", "head"), None),
            P(("seq", "head"), None),
            P(("seq", "head"), None),
            P(),
        ),
        out_specs=P(("seq", "head"), None),
        check_vma=False,
    )
```

```python
import jax
import jax.numpy as jnp
from jax import lax
from jax.experimental import pallas as pl
from jax.experimental.pallas import tpu as pltpu
from jax.sharding import PartitionSpec as P

E = 128
HEADS = 32
F32 = jnp.float32
BF16 = jnp.bfloat16
MESH = pl.DeviceIdType.MESH


def states_kernel(
    own, out,
    recv1, tot, recv2, tsum, sib, pbuf, recvy, rbuf, recvx, send3, recv3, send4, fin,
    s1, r1, s2, r2, ss, rs, sy, ry, sx, rx, s3, r3, s4, r4,
):
    g = lax.axis_index("seq")
    z = lax.axis_index("head")
    a, b = lax.div(z, 4), lax.rem(z, 4)
    core = lax.rem(g, 2)
    y = lax.rem(lax.div(g, 2), 4)
    x = lax.div(g, 8)
    other = g + 1 - 2 * core

    def step(v, d):
        return lax.rem(v + d, 4)

    def at_b(d):
        return {"seq": g, "head": a * 4 + step(b, d)}

    def at_a(d):
        return {"seq": g, "head": step(a, d) * 4 + b}

    def at_y(d):
        return {"seq": x * 8 + step(y, d) * 2 + core, "head": z}

    def at_x(d):
        return {"seq": step(x, d) * 8 + y * 2 + core, "head": z}

    def copy(src, dst, send, recv, where):
        return pltpu.make_async_remote_copy(
            src_ref=src, dst_ref=dst, send_sem=send, recv_sem=recv,
            device_id=where, device_id_type=MESH,
        )

    started = []

    def start(copies):
        for one in copies:
            one.start()
        started.extend(copies)
        return copies

    def arrive(copies):
        for one in copies:
            one.wait_recv()

    barrier = pltpu.get_barrier_semaphore()
    peers = [f(d) for f in (at_b, at_a, at_y, at_x) for d in (1, 2, 3)]
    peers.append({"seq": other, "head": z})
    for peer in peers:
        pl.semaphore_signal(barrier, inc=1, device_id=peer, device_id_type=MESH)
    pl.semaphore_wait(barrier, len(peers))

    def to_clusters(h):
        return start([
            copy(own.at[pl.ds(8 * step(b, d) + 4 * h, 4)], recv1.at[h, b],
                 s1.at[h, d - 1], r1.at[h, d - 1], at_b(d))
            for d in (1, 3, 2)
        ])

    def cluster_total(h):
        for i in range(4):
            mine = own[8 * b + 4 * h + i]
            recv1[h, b, i] = mine
            total = recv1[h, 0, i].astype(F32)
            for s in range(1, 4):
                total = total + recv1[h, s, i].astype(F32)
            tot[h, i] = total.astype(BF16)
        recv2[h, a] = tot[h, a]
        return start([
            copy(tot.at[h, step(a, d)], recv2.at[h, a],
                 s2.at[h, d - 1], r2.at[h, d - 1], at_a(d))
            for d in (2, 1, 3)
        ])

    def group_total(h):
        total = recv2[h, 0].astype(F32)
        for s in range(1, 4):
            total = total + recv2[h, s].astype(F32)
        tsum[h] = total.astype(BF16)
        return start([copy(tsum.at[h], sib.at[h], ss.at[h], rs.at[h], {"seq": other, "head": z})])

    def chip_total(h):
        both = (tsum[h].astype(F32) + sib[h].astype(F32)).astype(BF16)
        pbuf[h] = both
        recvy[h, y] = both
        return start([
            copy(pbuf.at[h], recvy.at[h, y], sy.at[h, d - 1], ry.at[h, d - 1], at_y(d))
            for d in (2, 1, 3)
        ])

    def row_total(h):
        total = recvy[h, 0].astype(F32)
        for s in range(1, 4):
            total = total + recvy[h, s].astype(F32)
        row = total.astype(BF16)
        rbuf[h] = row
        recvx[h, x] = row
        return start([
            copy(rbuf.at[h], recvx.at[h, x], sx.at[h, d - 1], rx.at[h, d - 1], at_x(d))
            for d in (2, 1, 3)
        ])

    def earlier_groups(h):
        state = jnp.where(core == 1, sib[h].astype(F32), 0.0)
        for s in range(3):
            state = state + jnp.where(s < y, recvy[h, s].astype(F32), 0.0)
        for s in range(3):
            state = state + jnp.where(s < x, recvx[h, s].astype(F32), 0.0)
        for s in range(4):
            send3[h, s] = state.astype(BF16)
            if s < 3:
                state = state + recv2[h, s].astype(F32)
        recv3[h, a] = send3[h, a]
        return start([
            copy(send3.at[h, step(a, d)], recv3.at[h, a],
                 s3.at[h, d - 1], r3.at[h, d - 1], at_a(d))
            for d in (2, 1, 3)
        ])

    def to_blocks(h):
        for i in range(4):
            state = recv3[h, i].astype(F32)
            for s in range(4):
                send4[h, s, i] = state.astype(BF16)
                if s < 3:
                    state = state + recv1[h, s, i].astype(F32)
        mine = pl.ds(8 * b + 4 * h, 4)
        fin[mine] = send4[h, b]
        return start([
            copy(send4.at[h, step(b, d)], fin.at[mine],
                 s4.at[h, d - 1], r4.at[h, d - 1], at_b(d))
            for d in (1, 3, 2)
        ])

    c1 = [to_clusters(0), to_clusters(1)]
    arrive(c1[0])
    c20 = cluster_total(0)
    arrive(c1[1])
    c21 = cluster_total(1)
    arrive(c20)
    cs0 = group_total(0)
    arrive(cs0)
    cy0 = chip_total(0)
    arrive(c21)
    cs1 = group_total(1)
    arrive(cy0)
    cx0 = row_total(0)
    arrive(cs1)
    cy1 = chip_total(1)
    arrive(cx0)
    c30 = earlier_groups(0)
    arrive(cy1)
    cx1 = row_total(1)
    arrive(cx1)
    c31 = earlier_groups(1)
    arrive(c30)
    c40 = to_blocks(0)
    arrive(c31)
    c41 = to_blocks(1)
    arrive(c40)
    arrive(c41)
    for one in started:
        one.wait_send()
    out[...] = fin[...]


def entering_states(own):
    def buf(*lead):
        return pltpu.VMEM((*lead, E, E), BF16)

    dma = pltpu.SemaphoreType.DMA
    three = [dma((2, 3)), dma((2, 3))]
    vmem = pl.BlockSpec(memory_space=pltpu.VMEM)
    return pl.pallas_call(
        states_kernel,
        out_shape=jax.ShapeDtypeStruct((HEADS, E, E), BF16),
        in_specs=[vmem],
        out_specs=vmem,
        scratch_shapes=[
            buf(2, 4, 4), buf(2, 4), buf(2, 4), buf(2), buf(2), buf(2), buf(2, 4), buf(2),
            buf(2, 4), buf(2, 4), buf(2, 4), buf(2, 4, 4), buf(HEADS),
            *three, *three, dma((2,)), dma((2,)), *three, *three, *three, *three,
        ],
        compiler_params=pltpu.CompilerParams(
            collective_id=0, has_side_effects=True, vmem_limit_bytes=40 * 1024 * 1024
        ),
    )(own)


def per_device(queries, keys, values, gain):
    block = queries.shape[0]
    q = queries.reshape(block, HEADS, E)
    k = keys.reshape(block, HEADS, E)
    v = values.reshape(block, HEADS, E)
    own = jnp.einsum("shd,she->hde", k, v, preferred_element_type=F32).astype(BF16)
    state = entering_states(own)
    lower = jnp.tril(jnp.ones((block, block), dtype=bool))
    scores = jnp.einsum("thd,shd->hts", q, k, preferred_element_type=F32)
    scores = jnp.where(lower[None], scores, 0.0).astype(BF16)
    inner = jnp.einsum("hts,shd->thd", scores, v, preferred_element_type=F32)
    outer = jnp.einsum("thd,hde->the", q, state, preferred_element_type=F32)
    home = (inner + outer).astype(BF16).reshape(block, HEADS * E).astype(F32)
    meansq = jnp.mean(home * home, axis=1, keepdims=True)
    return (home * lax.rsqrt(meansq + 1e-06) * gain[None, :]).astype(BF16)


def solution(mesh):
    return jax.shard_map(
        per_device,
        mesh=mesh,
        in_specs=(
            P(("seq", "head"), None),
            P(("seq", "head"), None),
            P(("seq", "head"), None),
            P(),
        ),
        out_specs=P(("seq", "head"), None),
        check_vma=False,
    )
```

```python
import jax
import jax.numpy as jnp
from jax import lax
from jax.experimental import pallas as pl
from jax.experimental.pallas import tpu as pltpu
from jax.sharding import PartitionSpec as P

E = 128
HEADS = 32
F32 = jnp.float32
BF16 = jnp.bfloat16
MESH = pl.DeviceIdType.MESH


def attention_kernel(
    q_hbm, k_hbm, v_hbm, out, scale,
    q, k, v, inner, squares, own, load, recv1, tot, recv2, tsum, sib, pbuf, recvy, rbuf, recvx, send3, recv3, send4, fin,
    s1, r1, s2, r2, ss, rs, sy, ry, sx, rx, s3, r3, s4, r4,
):
    g = lax.axis_index("seq")
    z = lax.axis_index("head")
    a, b = lax.div(z, 4), lax.rem(z, 4)
    core = lax.rem(g, 2)
    y = lax.rem(lax.div(g, 2), 4)
    x = lax.div(g, 8)
    other = g + 1 - 2 * core

    def step(v, d):
        return lax.rem(v + d, 4)

    def at_b(d):
        return {"seq": g, "head": a * 4 + step(b, d)}

    def at_a(d):
        return {"seq": g, "head": step(a, d) * 4 + b}

    def at_y(d):
        return {"seq": x * 8 + step(y, d) * 2 + core, "head": z}

    def at_x(d):
        return {"seq": step(x, d) * 8 + y * 2 + core, "head": z}

    def copy(src, dst, send, recv, where):
        return pltpu.make_async_remote_copy(
            src_ref=src, dst_ref=dst, send_sem=send, recv_sem=recv,
            device_id=where, device_id_type=MESH,
        )

    started = []

    def start(copies):
        for one in copies:
            one.start()
        started.extend(copies)
        return copies

    def arrive(copies):
        for one in copies:
            one.wait_recv()

    loads = [
        pltpu.make_async_copy(src, dst, load.at[i])
        for i, (src, dst) in enumerate(((k_hbm, k), (v_hbm, v), (q_hbm, q)))
    ]
    for one in loads:
        one.start()

    barrier = pltpu.get_barrier_semaphore()
    peers = [f(d) for f in (at_b, at_a, at_y, at_x) for d in (1, 2, 3)]
    peers.append({"seq": other, "head": z})
    for peer in peers:
        pl.semaphore_signal(barrier, inc=1, device_id=peer, device_id_type=MESH)

    def cols(head):
        return pl.ds(pl.multiple_of(head * E, E), E)

    def own_states(h):
        def body(j, carry):
            for i in range(4):
                head = 8 * j + 4 * h + i
                state = lax.dot_general(
                    k[:, cols(head)], v[:, cols(head)], (((0,), (0,)), ((), ())),
                    preferred_element_type=F32,
                )
                own[head] = state.astype(BF16)
            return carry

        lax.fori_loop(0, 4, body, 0)

    def inner_products():
        lower = lax.broadcasted_iota(jnp.int32, (E, E), 0) >= lax.broadcasted_iota(
            jnp.int32, (E, E), 1
        )

        def body(j, carry):
            for i in range(4):
                at = cols(4 * j + i)
                scores = lax.dot_general(
                    q[:, at], k[:, at], (((1,), (1,)), ((), ())), preferred_element_type=F32
                )
                scores = jnp.where(lower, scores, 0.0).astype(BF16)
                inner[:, at] = jnp.dot(scores, v[:, at], preferred_element_type=F32)
            return carry

        lax.fori_loop(0, HEADS // 4, body, 0)
        squares[...] = jnp.zeros_like(squares)

    def outer_products(h):
        def body(j, carry):
            total = squares[...]
            for i in range(4):
                head = 8 * j + 4 * h + i
                at = cols(head)
                outer = jnp.dot(q[:, at], fin[head], preferred_element_type=F32)
                attended = (inner[:, at] + outer).astype(BF16)
                out[:, at] = attended
                wide = attended.astype(F32)
                total = total + wide * wide
            squares[...] = total
            return carry

        lax.fori_loop(0, 4, body, 0)

    loads[0].wait()
    loads[1].wait()
    own_states(0)
    pl.semaphore_wait(barrier, len(peers))

    def to_clusters(h):
        return start([
            copy(own.at[pl.ds(8 * step(b, d) + 4 * h, 4)], recv1.at[h, b],
                 s1.at[h, d - 1], r1.at[h, d - 1], at_b(d))
            for d in (1, 3, 2)
        ])

    def cluster_total(h):
        for i in range(4):
            mine = own[8 * b + 4 * h + i]
            recv1[h, b, i] = mine
            total = recv1[h, 0, i].astype(F32)
            for s in range(1, 4):
                total = total + recv1[h, s, i].astype(F32)
            tot[h, i] = total.astype(BF16)
        recv2[h, a] = tot[h, a]
        return start([
            copy(tot.at[h, step(a, d)], recv2.at[h, a],
                 s2.at[h, d - 1], r2.at[h, d - 1], at_a(d))
            for d in (2, 1, 3)
        ])

    def group_total(h):
        total = recv2[h, 0].astype(F32)
        for s in range(1, 4):
            total = total + recv2[h, s].astype(F32)
        tsum[h] = total.astype(BF16)
        return start([copy(tsum.at[h], sib.at[h], ss.at[h], rs.at[h], {"seq": other, "head": z})])

    def chip_total(h):
        both = (tsum[h].astype(F32) + sib[h].astype(F32)).astype(BF16)
        pbuf[h] = both
        recvy[h, y] = both
        return start([
            copy(pbuf.at[h], recvy.at[h, y], sy.at[h, d - 1], ry.at[h, d - 1], at_y(d))
            for d in (2, 1, 3)
        ])

    def row_total(h):
        total = recvy[h, 0].astype(F32)
        for s in range(1, 4):
            total = total + recvy[h, s].astype(F32)
        row = total.astype(BF16)
        rbuf[h] = row
        recvx[h, x] = row
        return start([
            copy(rbuf.at[h], recvx.at[h, x], sx.at[h, d - 1], rx.at[h, d - 1], at_x(d))
            for d in (2, 1, 3)
        ])

    def earlier_groups(h):
        state = jnp.where(core == 1, sib[h].astype(F32), 0.0)
        for s in range(3):
            state = state + jnp.where(s < y, recvy[h, s].astype(F32), 0.0)
        for s in range(3):
            state = state + jnp.where(s < x, recvx[h, s].astype(F32), 0.0)
        for s in range(4):
            send3[h, s] = state.astype(BF16)
            if s < 3:
                state = state + recv2[h, s].astype(F32)
        recv3[h, a] = send3[h, a]
        return start([
            copy(send3.at[h, step(a, d)], recv3.at[h, a],
                 s3.at[h, d - 1], r3.at[h, d - 1], at_a(d))
            for d in (2, 1, 3)
        ])

    def to_blocks(h):
        for i in range(4):
            state = recv3[h, i].astype(F32)
            for s in range(4):
                send4[h, s, i] = state.astype(BF16)
                if s < 3:
                    state = state + recv1[h, s, i].astype(F32)
        mine = pl.ds(8 * b + 4 * h, 4)
        fin[mine] = send4[h, b]
        return start([
            copy(send4.at[h, step(b, d)], fin.at[mine],
                 s4.at[h, d - 1], r4.at[h, d - 1], at_b(d))
            for d in (1, 3, 2)
        ])

    c1 = [to_clusters(0)]
    own_states(1)
    c1.append(to_clusters(1))
    loads[2].wait()
    inner_products()
    arrive(c1[0])
    c20 = cluster_total(0)
    arrive(c1[1])
    c21 = cluster_total(1)
    arrive(c20)
    cs0 = group_total(0)
    arrive(cs0)
    cy0 = chip_total(0)
    arrive(c21)
    cs1 = group_total(1)
    arrive(cy0)
    cx0 = row_total(0)
    arrive(cs1)
    cy1 = chip_total(1)
    arrive(cx0)
    c30 = earlier_groups(0)
    arrive(cy1)
    cx1 = row_total(1)
    arrive(cx1)
    c31 = earlier_groups(1)
    arrive(c30)
    c40 = to_blocks(0)
    arrive(c31)
    c41 = to_blocks(1)
    arrive(c40)
    outer_products(0)
    arrive(c41)
    outer_products(1)
    meansq = jnp.sum(squares[...], axis=1, keepdims=True) * (1.0 / (HEADS * E))
    scale[...] = jnp.broadcast_to(lax.rsqrt(meansq + 1e-06), scale.shape)
    for one in started:
        one.wait_send()


def per_device(queries, keys, values, gain):
    rows, feat = queries.shape

    def buf(*lead):
        return pltpu.VMEM((*lead, E, E), BF16)

    dma = pltpu.SemaphoreType.DMA
    three = [dma((2, 3)), dma((2, 3))]
    vmem = pl.BlockSpec(memory_space=pltpu.VMEM)
    hbm = pl.BlockSpec(memory_space=pltpu.HBM)
    tokens = pltpu.VMEM((rows, feat), BF16)
    attended, scale = pl.pallas_call(
        attention_kernel,
        out_shape=(
            jax.ShapeDtypeStruct((rows, feat), BF16),
            jax.ShapeDtypeStruct((rows, E), F32),
        ),
        in_specs=[hbm] * 3,
        out_specs=(vmem, vmem),
        scratch_shapes=[
            tokens, tokens, tokens, pltpu.VMEM((rows, feat), F32), pltpu.VMEM((rows, E), F32),
            buf(HEADS), dma((3,)),
            buf(2, 4, 4), buf(2, 4), buf(2, 4), buf(2), buf(2), buf(2), buf(2, 4), buf(2),
            buf(2, 4), buf(2, 4), buf(2, 4), buf(2, 4, 4), buf(HEADS),
            *three, *three, dma((2,)), dma((2,)), *three, *three, *three, *three,
        ],
        compiler_params=pltpu.CompilerParams(
            collective_id=0, has_side_effects=True, vmem_limit_bytes=65600000
        ),
    )(queries, keys, values)
    return (attended.astype(F32) * scale[:, :1] * gain[None, :]).astype(BF16)


def solution(mesh):
    return jax.shard_map(
        per_device,
        mesh=mesh,
        in_specs=(
            P(("seq", "head"), None),
            P(("seq", "head"), None),
            P(("seq", "head"), None),
            P(),
        ),
        out_specs=P(("seq", "head"), None),
        check_vma=False,
    )
```

```python
import jax
import jax.numpy as jnp
from jax import lax
from jax.experimental import pallas as pl
from jax.experimental.pallas import tpu as pltpu
from jax.sharding import PartitionSpec as P

E = 128
HEADS = 32
F32 = jnp.float32
BF16 = jnp.bfloat16
MESH = pl.DeviceIdType.MESH


def attention_kernel(
    q_hbm, k_hbm, v_hbm, gain, out,
    q, k, v, inner, squares, own, load,
    ra, psum, rb, ctot, rc, tsum, sib, pbuf, recvy, rbuf, recvx,
    sendc, enter, sendb, pair_enter, senda, fin,
    sa, qa, sb, qb, sc, qc, ss, rs, sy, ry, sx, rx, sc2, qc2, sb2, qb2, sa2, qa2,
):
    g = lax.axis_index("seq")
    z = lax.axis_index("head")
    a, b = lax.div(z, 4), lax.rem(z, 4)
    p, e = lax.div(b, 2), lax.rem(b, 2)
    core = lax.rem(g, 2)
    y = lax.rem(lax.div(g, 2), 4)
    x = lax.div(g, 8)
    other = g + 1 - 2 * core

    def step(v, d):
        return lax.rem(v + d, 4)

    at_e = {"seq": g, "head": z + 1 - 2 * e}
    at_p = {"seq": g, "head": z + 2 - 4 * p}
    at_core = {"seq": other, "head": z}

    def at_a(d):
        return {"seq": g, "head": step(a, d) * 4 + b}

    def at_y(d):
        return {"seq": x * 8 + step(y, d) * 2 + core, "head": z}

    def at_x(d):
        return {"seq": step(x, d) * 8 + y * 2 + core, "head": z}

    def copy(src, dst, send, recv, where):
        return pltpu.make_async_remote_copy(
            src_ref=src, dst_ref=dst, send_sem=send, recv_sem=recv,
            device_id=where, device_id_type=MESH,
        )

    started = []

    def start(copies):
        for one in copies:
            one.start()
        started.extend(copies)
        return copies

    def arrive(copies):
        for one in copies:
            one.wait_recv()

    loads = [
        pltpu.make_async_copy(src, dst, load.at[i])
        for i, (src, dst) in enumerate(((k_hbm, k), (v_hbm, v), (q_hbm, q)))
    ]
    for one in loads:
        one.start()

    barrier = pltpu.get_barrier_semaphore()
    peers = [f(d) for f in (at_a, at_y, at_x) for d in (1, 2, 3)]
    peers.extend([at_e, at_p, at_core])
    for peer in peers:
        pl.semaphore_signal(barrier, inc=1, device_id=peer, device_id_type=MESH)

    def cols(head):
        return pl.ds(pl.multiple_of(head * E, E), E)

    def own_states(h):
        def body(j, carry):
            for i in range(4):
                head = 16 * h + 4 * j + i
                state = lax.dot_general(
                    k[:, cols(head)], v[:, cols(head)], (((0,), (0,)), ((), ())),
                    preferred_element_type=F32,
                )
                own[head] = state.astype(BF16)
            return carry

        lax.fori_loop(0, 4, body, 0)

    def inner_products():
        lower = lax.broadcasted_iota(jnp.int32, (E, E), 0) >= lax.broadcasted_iota(
            jnp.int32, (E, E), 1
        )

        def body(j, carry):
            for i in range(4):
                at = cols(4 * j + i)
                scores = lax.dot_general(
                    q[:, at], k[:, at], (((1,), (1,)), ((), ())), preferred_element_type=F32
                )
                scores = jnp.where(lower, scores, 0.0).astype(BF16)
                inner[:, at] = jnp.dot(scores, v[:, at], preferred_element_type=F32)
            return carry

        lax.fori_loop(0, HEADS // 4, body, 0)
        squares[...] = jnp.zeros_like(squares)

    def outer_products(h):
        def body(j, carry):
            total = squares[...]
            for i in range(4):
                head = 16 * h + 4 * j + i
                at = cols(head)
                outer = jnp.dot(q[:, at], fin[head], preferred_element_type=F32)
                attended = (inner[:, at] + outer).astype(BF16)
                out[:, at] = attended
                wide = attended.astype(F32)
                total = total + wide * wide
            squares[...] = total
            return carry

        lax.fori_loop(0, 4, body, 0)

    loads[0].wait()
    loads[1].wait()
    own_states(0)
    pl.semaphore_wait(barrier, len(peers))

    def to_pairs(h):
        return start([copy(own.at[pl.ds(16 * h + 8 * (1 - e), 8)], ra.at[h], sa.at[h], qa.at[h], at_e)])

    def pair_total(h):
        for i in range(8):
            mine = own[16 * h + 8 * e + i].astype(F32)
            psum[h, i] = (mine + ra[h, i].astype(F32)).astype(BF16)
        return start([copy(psum.at[h, pl.ds(4 * (1 - p), 4)], rb.at[h], sb.at[h], qb.at[h], at_p)])

    def cluster_total(h):
        for i in range(4):
            total = psum[h, 4 * p + i].astype(F32) + rb[h, i].astype(F32)
            ctot[h, i] = total.astype(BF16)
        rc[h, a] = ctot[h, a]
        return start([
            copy(ctot.at[h, step(a, d)], rc.at[h, a],
                 sc.at[h, d - 1], qc.at[h, d - 1], at_a(d))
            for d in (2, 1, 3)
        ])

    def group_total(h):
        total = rc[h, 0].astype(F32)
        for s in range(1, 4):
            total = total + rc[h, s].astype(F32)
        tsum[h] = total.astype(BF16)
        return start([copy(tsum.at[h], sib.at[h], ss.at[h], rs.at[h], at_core)])

    def chip_total(h):
        both = (tsum[h].astype(F32) + sib[h].astype(F32)).astype(BF16)
        pbuf[h] = both
        recvy[h, y] = both
        return start([
            copy(pbuf.at[h], recvy.at[h, y], sy.at[h, d - 1], ry.at[h, d - 1], at_y(d))
            for d in (2, 1, 3)
        ])

    def row_total(h):
        total = recvy[h, 0].astype(F32)
        for s in range(1, 4):
            total = total + recvy[h, s].astype(F32)
        row = total.astype(BF16)
        rbuf[h] = row
        recvx[h, x] = row
        return start([
            copy(rbuf.at[h], recvx.at[h, x], sx.at[h, d - 1], rx.at[h, d - 1], at_x(d))
            for d in (2, 1, 3)
        ])

    def earlier_groups(h):
        state = jnp.where(core == 1, sib[h].astype(F32), 0.0)
        for s in range(3):
            state = state + jnp.where(s < y, recvy[h, s].astype(F32), 0.0)
        for s in range(3):
            state = state + jnp.where(s < x, recvx[h, s].astype(F32), 0.0)
        for s in range(4):
            sendc[h, s] = state.astype(BF16)
            if s < 3:
                state = state + rc[h, s].astype(F32)
        enter[h, a] = sendc[h, a]
        return start([
            copy(sendc.at[h, step(a, d)], enter.at[h, a],
                 sc2.at[h, d - 1], qc2.at[h, d - 1], at_a(d))
            for d in (2, 1, 3)
        ])

    def back_to_pairs(h):
        for i in range(4):
            state = enter[h, i].astype(F32)
            first = psum[h, 4 * p + i].astype(F32)
            sendb[h, i] = (state + jnp.where(p == 0, first, 0.0)).astype(BF16)
            second = rb[h, i].astype(F32)
            pair_enter[h, 4 * p + i] = (state + jnp.where(p == 1, second, 0.0)).astype(BF16)
        return start([
            copy(sendb.at[h], pair_enter.at[h, pl.ds(4 * p, 4)], sb2.at[h], qb2.at[h], at_p)
        ])

    def back_to_blocks(h):
        for i in range(8):
            head = 16 * h + 8 * e + i
            state = pair_enter[h, i].astype(F32)
            first = own[head].astype(F32)
            senda[h, i] = (state + jnp.where(e == 0, first, 0.0)).astype(BF16)
            second = ra[h, i].astype(F32)
            fin[head] = (state + jnp.where(e == 1, second, 0.0)).astype(BF16)
        return start([
            copy(senda.at[h], fin.at[pl.ds(16 * h + 8 * e, 8)], sa2.at[h], qa2.at[h], at_e)
        ])

    ca0 = to_pairs(0)
    own_states(1)
    ca1 = to_pairs(1)
    arrive(ca0)
    cb0 = pair_total(0)
    loads[2].wait()
    inner_products()
    arrive(ca1)
    cb1 = pair_total(1)
    arrive(cb0)
    cc0 = cluster_total(0)
    arrive(cb1)
    cc1 = cluster_total(1)
    arrive(cc0)
    cs0 = group_total(0)
    arrive(cs0)
    cy0 = chip_total(0)
    arrive(cc1)
    cs1 = group_total(1)
    arrive(cy0)
    cx0 = row_total(0)
    arrive(cs1)
    cy1 = chip_total(1)
    arrive(cx0)
    c30 = earlier_groups(0)
    arrive(cy1)
    cx1 = row_total(1)
    arrive(cx1)
    c31 = earlier_groups(1)
    arrive(c30)
    cp0 = back_to_pairs(0)
    arrive(c31)
    cp1 = back_to_pairs(1)
    arrive(cp0)
    c40 = back_to_blocks(0)
    arrive(cp1)
    c41 = back_to_blocks(1)
    arrive(c40)
    outer_products(0)
    arrive(c41)
    outer_products(1)
    meansq = jnp.sum(squares[...], axis=1, keepdims=True) * (1.0 / (HEADS * E))
    scale = lax.rsqrt(meansq + 1e-06)

    def norm(j, carry):
        for i in range(4):
            at = cols(4 * j + i)
            out[:, at] = (out[:, at].astype(F32) * scale * gain[:, at]).astype(BF16)
        return carry

    lax.fori_loop(0, HEADS // 4, norm, 0)
    for one in started:
        one.wait_send()


def per_device(queries, keys, values, gain):
    rows, feat = queries.shape

    def buf(*lead):
        return pltpu.VMEM((*lead, E, E), BF16)

    dma = pltpu.SemaphoreType.DMA
    one = [dma((2,)), dma((2,))]
    three = [dma((2, 3)), dma((2, 3))]
    vmem = pl.BlockSpec(memory_space=pltpu.VMEM)
    hbm = pl.BlockSpec(memory_space=pltpu.HBM)
    tokens = pltpu.VMEM((rows, feat), BF16)
    return pl.pallas_call(
        attention_kernel,
        out_shape=jax.ShapeDtypeStruct((rows, feat), BF16),
        in_specs=[hbm, hbm, hbm, vmem],
        out_specs=vmem,
        scratch_shapes=[
            tokens, tokens, tokens, pltpu.VMEM((rows, feat), F32), pltpu.VMEM((rows, E), F32),
            buf(HEADS), dma((3,)),
            buf(2, 8), buf(2, 8), buf(2, 4), buf(2, 4), buf(2, 4),
            buf(2), buf(2), buf(2), buf(2, 4), buf(2), buf(2, 4),
            buf(2, 4), buf(2, 4), buf(2, 4), buf(2, 8), buf(2, 8), buf(HEADS),
            *one, *one, *three, *one, *three, *three, *three, *one, *one,
        ],
        compiler_params=pltpu.CompilerParams(
            collective_id=0, has_side_effects=True, vmem_limit_bytes=65600000
        ),
    )(queries, keys, values, gain.reshape(1, feat))


def solution(mesh):
    return jax.shard_map(
        per_device,
        mesh=mesh,
        in_specs=(
            P(("seq", "head"), None),
            P(("seq", "head"), None),
            P(("seq", "head"), None),
            P(),
        ),
        out_specs=P(("seq", "head"), None),
        check_vma=False,
    )
```

```python
import jax
import jax.numpy as jnp
from jax import lax
from jax.experimental import pallas as pl
from jax.experimental.pallas import tpu as pltpu
from jax.sharding import PartitionSpec as P

E = 128
HEADS = 32
PIECES = 4
ROWS = 64
F32 = jnp.float32
BF16 = jnp.bfloat16
MESH = pl.DeviceIdType.MESH


def attention_kernel(
    q_hbm, k_hbm, v_hbm, gain, out,
    q, k, v, inner, squares, own, load,
    ra, psum, rb, ctot, rc, tsum, sib, pbuf, recvy, rbuf, recvx,
    sendc, enter, sendb, pair_enter, senda, fin,
    sa, qa, sb, qb, sc, qc, ss, rs, sy, ry, sx, rx, sc2, qc2, sb2, qb2, sa2, qa2,
):
    g = lax.axis_index("seq")
    z = lax.axis_index("head")
    a, b = lax.div(z, 4), lax.rem(z, 4)
    p, e = lax.div(b, 2), lax.rem(b, 2)
    core = lax.rem(g, 2)
    y = lax.rem(lax.div(g, 2), 4)
    x = lax.div(g, 8)
    other = g + 1 - 2 * core

    def step(v, d):
        return lax.rem(v + d, 4)

    at_e = {"seq": g, "head": z + 1 - 2 * e}
    at_p = {"seq": g, "head": z + 2 - 4 * p}
    at_core = {"seq": other, "head": z}

    def at_a(d):
        return {"seq": g, "head": step(a, d) * 4 + b}

    def at_y(d):
        return {"seq": x * 8 + step(y, d) * 2 + core, "head": z}

    def at_x(d):
        return {"seq": step(x, d) * 8 + y * 2 + core, "head": z}

    def copy(src, dst, send, recv, where):
        return pltpu.make_async_remote_copy(
            src_ref=src, dst_ref=dst, send_sem=send, recv_sem=recv,
            device_id=where, device_id_type=MESH,
        )

    started = []

    def start(copies):
        for one in copies:
            one.start()
        started.extend(copies)
        return copies

    def arrive(copies):
        for one in copies:
            one.wait_recv()

    barrier = pltpu.get_barrier_semaphore()
    peers = [f(d) for f in (at_a, at_y, at_x) for d in (1, 2, 3)]
    peers.extend([at_e, at_p, at_core])
    for peer in peers:
        pl.semaphore_signal(barrier, inc=1, device_id=peer, device_id_type=MESH)

    wide = 8 * E
    loads = [
        pltpu.make_async_copy(
            src.at[:, pl.ds(h * wide, wide)], dst.at[:, pl.ds(h * wide, wide)], load.at[2 * h + i]
        )
        for h in range(PIECES)
        for i, (src, dst) in enumerate(((k_hbm, k), (v_hbm, v)))
    ]
    loads.append(pltpu.make_async_copy(q_hbm, q, load.at[2 * PIECES]))
    for one in loads:
        one.start()

    def cols(head):
        return pl.ds(pl.multiple_of(head * E, E), E)

    def own_states(h):
        loads[2 * h].wait()
        loads[2 * h + 1].wait()
        for head in range(8 * h, 8 * h + 8):
            at = pl.ds(head * E, E)
            state = lax.dot_general(
                k[:, at], v[:, at], (((0,), (0,)), ((), ())), preferred_element_type=F32
            )
            own[pl.ds(2 * head, 2)] = state.astype(BF16).reshape(2, ROWS, E)

    def inner_products(h):
        lower = lax.broadcasted_iota(jnp.int32, (E, E), 0) >= lax.broadcasted_iota(
            jnp.int32, (E, E), 1
        )

        def body(j, carry):
            for i in range(4):
                at = cols(8 * h + 4 * j + i)
                scores = lax.dot_general(
                    q[:, at], k[:, at], (((1,), (1,)), ((), ())), preferred_element_type=F32
                )
                scores = jnp.where(lower, scores, 0.0).astype(BF16)
                inner[:, at] = jnp.dot(scores, v[:, at], preferred_element_type=F32)
            return carry

        lax.fori_loop(0, 2, body, 0)

    def outer_products(h):
        def body(j, carry):
            total = squares[...]
            for i in range(4):
                head = 8 * h + 4 * j + i
                at = cols(head)
                state = fin[pl.ds(2 * head, 2)].reshape(E, E)
                outer = jnp.dot(q[:, at], state, preferred_element_type=F32)
                attended = (inner[:, at] + outer).astype(BF16)
                out[:, at] = attended
                wide = attended.astype(F32)
                total = total + wide * wide
            squares[...] = total
            return carry

        lax.fori_loop(0, 2, body, 0)

    own_states(0)
    pl.semaphore_wait(barrier, len(peers))

    def to_pairs(h):
        return start([copy(own.at[pl.ds(16 * h + 8 * (1 - e), 8)], ra.at[h], sa.at[h], qa.at[h], at_e)])

    def pair_total(h):
        for i in range(8):
            mine = own[16 * h + 8 * e + i].astype(F32)
            psum[h, i] = (mine + ra[h, i].astype(F32)).astype(BF16)
        return start([copy(psum.at[h, pl.ds(4 * (1 - p), 4)], rb.at[h], sb.at[h], qb.at[h], at_p)])

    def cluster_total(h):
        for i in range(4):
            total = psum[h, 4 * p + i].astype(F32) + rb[h, i].astype(F32)
            ctot[h, i] = total.astype(BF16)
        rc[h, a] = ctot[h, a]
        return start([
            copy(ctot.at[h, step(a, d)], rc.at[h, a],
                 sc.at[h, d - 1], qc.at[h, d - 1], at_a(d))
            for d in (2, 1, 3)
        ])

    def group_total(h):
        total = rc[h, 0].astype(F32)
        for s in range(1, 4):
            total = total + rc[h, s].astype(F32)
        tsum[h] = total.astype(BF16)
        return start([copy(tsum.at[h], sib.at[h], ss.at[h], rs.at[h], at_core)])

    def chip_total(h):
        both = (tsum[h].astype(F32) + sib[h].astype(F32)).astype(BF16)
        pbuf[h] = both
        recvy[h, y] = both
        return start([
            copy(pbuf.at[h], recvy.at[h, y], sy.at[h, d - 1], ry.at[h, d - 1], at_y(d))
            for d in (2, 1, 3)
        ])

    def row_total(h):
        total = recvy[h, 0].astype(F32)
        for s in range(1, 4):
            total = total + recvy[h, s].astype(F32)
        row = total.astype(BF16)
        rbuf[h] = row
        recvx[h, x] = row
        return start([
            copy(rbuf.at[h], recvx.at[h, x], sx.at[h, d - 1], rx.at[h, d - 1], at_x(d))
            for d in (2, 1, 3)
        ])

    def earlier_groups(h):
        state = jnp.where(core == 1, sib[h].astype(F32), 0.0)
        for s in range(3):
            state = state + jnp.where(s < y, recvy[h, s].astype(F32), 0.0)
        for s in range(3):
            state = state + jnp.where(s < x, recvx[h, s].astype(F32), 0.0)
        for s in range(4):
            sendc[h, s] = state.astype(BF16)
            if s < 3:
                state = state + rc[h, s].astype(F32)
        enter[h, a] = sendc[h, a]
        return start([
            copy(sendc.at[h, step(a, d)], enter.at[h, a],
                 sc2.at[h, d - 1], qc2.at[h, d - 1], at_a(d))
            for d in (2, 1, 3)
        ])

    def back_to_pairs(h):
        for i in range(4):
            state = enter[h, i].astype(F32)
            first = psum[h, 4 * p + i].astype(F32)
            sendb[h, i] = (state + jnp.where(p == 0, first, 0.0)).astype(BF16)
            second = rb[h, i].astype(F32)
            pair_enter[h, 4 * p + i] = (state + jnp.where(p == 1, second, 0.0)).astype(BF16)
        return start([
            copy(sendb.at[h], pair_enter.at[h, pl.ds(4 * p, 4)], sb2.at[h], qb2.at[h], at_p)
        ])

    def back_to_blocks(h):
        for i in range(8):
            head = 16 * h + 8 * e + i
            state = pair_enter[h, i].astype(F32)
            first = own[head].astype(F32)
            senda[h, i] = (state + jnp.where(e == 0, first, 0.0)).astype(BF16)
            second = ra[h, i].astype(F32)
            fin[head] = (state + jnp.where(e == 1, second, 0.0)).astype(BF16)
        return start([
            copy(senda.at[h], fin.at[pl.ds(16 * h + 8 * e, 8)], sa2.at[h], qa2.at[h], at_e)
        ])

    steps = [
        (pair_total, 4.5), (cluster_total, 10.0), (group_total, 19.0), (chip_total, 21.0),
        (row_total, 24.0), (earlier_groups, 27.5), (back_to_pairs, 36.5),
        (back_to_blocks, 42.0), (outer_products, 47.0),
    ]
    order = sorted(
        (when + 4.0 * h, h, n) for n, (_, when) in enumerate(steps) for h in range(PIECES)
    )
    flying = {0: to_pairs(0)}
    own_states(1)
    flying[1] = to_pairs(1)
    own_states(2)
    own_states(3)
    squares[...] = jnp.zeros_like(squares)
    loads[-1].wait()
    for _, h, n in order:
        arrive(flying[h])
        flying[h] = steps[n][0](h)
        if n == 0:
            if h + 2 < PIECES:
                flying[h + 2] = to_pairs(h + 2)
            inner_products(h)
    meansq = jnp.sum(squares[...], axis=1, keepdims=True) * (1.0 / (HEADS * E))
    scale = lax.rsqrt(meansq + 1e-06)

    def norm(j, carry):
        for i in range(4):
            at = cols(4 * j + i)
            out[:, at] = (out[:, at].astype(F32) * scale * gain[:, at]).astype(BF16)
        return carry

    lax.fori_loop(0, HEADS // 4, norm, 0)
    for one in started:
        one.wait_send()


def per_device(queries, keys, values, gain):
    rows, feat = queries.shape

    def buf(*lead):
        return pltpu.VMEM((*lead, ROWS, E), BF16)

    dma = pltpu.SemaphoreType.DMA
    n = PIECES
    one = [dma((n,)), dma((n,))]
    three = [dma((n, 3)), dma((n, 3))]
    vmem = pl.BlockSpec(memory_space=pltpu.VMEM)
    hbm = pl.BlockSpec(memory_space=pltpu.HBM)
    tokens = pltpu.VMEM((rows, feat), BF16)
    return pl.pallas_call(
        attention_kernel,
        out_shape=jax.ShapeDtypeStruct((rows, feat), BF16),
        in_specs=[hbm, hbm, hbm, vmem],
        out_specs=vmem,
        scratch_shapes=[
            tokens, tokens, tokens, pltpu.VMEM((rows, feat), F32), pltpu.VMEM((rows, E), F32),
            buf(2 * HEADS), dma((2 * PIECES + 1,)),
            buf(n, 8), buf(n, 8), buf(n, 4), buf(n, 4), buf(n, 4),
            buf(n), buf(n), buf(n), buf(n, 4), buf(n), buf(n, 4),
            buf(n, 4), buf(n, 4), buf(n, 4), buf(n, 8), buf(n, 8), buf(2 * HEADS),
            *one, *one, *three, *one, *three, *three, *three, *one, *one,
        ],
        compiler_params=pltpu.CompilerParams(
            collective_id=0, has_side_effects=True, vmem_limit_bytes=65600000
        ),
    )(queries, keys, values, gain.reshape(1, feat))


def solution(mesh):
    return jax.shard_map(
        per_device,
        mesh=mesh,
        in_specs=(
            P(("seq", "head"), None),
            P(("seq", "head"), None),
            P(("seq", "head"), None),
            P(),
        ),
        out_specs=P(("seq", "head"), None),
        check_vma=False,
    )
```

```python
import jax
import jax.numpy as jnp
from jax import lax
from jax.experimental import pallas as pl
from jax.experimental.pallas import tpu as pltpu
from jax.sharding import PartitionSpec as P

E = 128
HEADS = 32
PIECES = 4
ROWS = 64
F32 = jnp.float32
BF16 = jnp.bfloat16
MESH = pl.DeviceIdType.MESH


def attention_kernel(
    q_hbm, k_hbm, v_hbm, out_hbm,
    q, k, v, inner, out, own, load, leave,
    ra, psum, rb, ctot, rc, tsum, recvy, rbuf, recvx,
    sendc, enter, sendb, pair_enter, senda, fin,
    sa, qa, sb, qb, sc, qc, sy, ry, sx, rx, sc2, qc2, sb2, qb2, sa2, qa2,
):
    g = lax.axis_index("seq")
    z = lax.axis_index("head")
    a, b = lax.div(z, 4), lax.rem(z, 4)
    p, e = lax.div(b, 2), lax.rem(b, 2)
    x = lax.div(g, 8)

    def step(v, d):
        return lax.rem(v + d, 4)

    at_e = {"seq": g, "head": z + 1 - 2 * e}
    at_p = {"seq": g, "head": z + 2 - 4 * p}

    def at_a(d):
        return {"seq": g, "head": step(a, d) * 4 + b}

    row_at = lax.rem(g, 8)

    def at_row(d):
        return {"seq": x * 8 + lax.rem(row_at + d, 8), "head": z}

    def at_x(d):
        return {"seq": step(x, d) * 8 + row_at, "head": z}

    def copy(src, dst, send, recv, where):
        return pltpu.make_async_remote_copy(
            src_ref=src, dst_ref=dst, send_sem=send, recv_sem=recv,
            device_id=where, device_id_type=MESH,
        )

    started = []

    def start(copies):
        for one in copies:
            one.start()
        started.extend(copies)
        return copies

    def arrive(copies):
        for one in copies:
            one.wait_recv()

    barrier = pltpu.get_barrier_semaphore()
    peers = [f(d) for f in (at_a, at_x) for d in (1, 2, 3)]
    peers.extend([at_e, at_p])
    peers.extend(at_row(d) for d in range(1, 8))
    for peer in peers:
        pl.semaphore_signal(barrier, inc=1, device_id=peer, device_id_type=MESH)

    wide = 8 * E
    loads = [
        pltpu.make_async_copy(
            src.at[:, pl.ds(h * wide, wide)], dst.at[:, pl.ds(h * wide, wide)], load.at[2 * h + i]
        )
        for h in range(PIECES)
        for i, (src, dst) in enumerate(((k_hbm, k), (v_hbm, v)))
    ]
    loads.append(pltpu.make_async_copy(q_hbm, q, load.at[2 * PIECES]))
    for one in loads:
        one.start()

    def cols(head):
        return pl.ds(pl.multiple_of(head * E, E), E)

    def own_states(h):
        loads[2 * h].wait()
        loads[2 * h + 1].wait()
        for head in range(8 * h, 8 * h + 8):
            at = pl.ds(head * E, E)
            state = lax.dot_general(
                k[:, at], v[:, at], (((0,), (0,)), ((), ())), preferred_element_type=F32
            )
            own[pl.ds(2 * head, 2)] = state.astype(BF16).reshape(2, ROWS, E)

    def inner_products(h):
        lower = lax.broadcasted_iota(jnp.int32, (E, E), 0) >= lax.broadcasted_iota(
            jnp.int32, (E, E), 1
        )

        def body(j, carry):
            for i in range(4):
                at = cols(8 * h + 4 * j + i)
                scores = lax.dot_general(
                    q[:, at], k[:, at], (((1,), (1,)), ((), ())), preferred_element_type=F32
                )
                scores = jnp.where(lower, scores, 0.0).astype(BF16)
                inner[:, at] = jnp.dot(scores, v[:, at], preferred_element_type=F32)
            return carry

        lax.fori_loop(0, 2, body, 0)

    def outer_products(h):
        def body(j, carry):
            for i in range(4):
                head = 8 * h + 4 * j + i
                at = cols(head)
                state = fin[pl.ds(2 * head, 2)].reshape(E, E)
                outer = jnp.dot(q[:, at], state, preferred_element_type=F32)
                out[:, at] = (inner[:, at] + outer).astype(BF16)
            return carry

        lax.fori_loop(0, 2, body, 0)
        mine = pl.ds(h * wide, wide)
        leaving = pltpu.make_async_copy(out.at[:, mine], out_hbm.at[:, mine], leave.at[h])
        leaving.start()
        return leaving

    own_states(0)
    pl.semaphore_wait(barrier, len(peers))

    def to_pairs(h):
        return start([copy(own.at[pl.ds(16 * h + 8 * (1 - e), 8)], ra.at[h], sa.at[h], qa.at[h], at_e)])

    def pair_total(h):
        for i in range(8):
            mine = own[16 * h + 8 * e + i].astype(F32)
            psum[h, i] = (mine + ra[h, i].astype(F32)).astype(BF16)
        return start([copy(psum.at[h, pl.ds(4 * (1 - p), 4)], rb.at[h], sb.at[h], qb.at[h], at_p)])

    def cluster_total(h):
        for i in range(4):
            total = psum[h, 4 * p + i].astype(F32) + rb[h, i].astype(F32)
            ctot[h, i] = total.astype(BF16)
        rc[h, a] = ctot[h, a]
        return start([
            copy(ctot.at[h, step(a, d)], rc.at[h, a],
                 sc.at[h, d - 1], qc.at[h, d - 1], at_a(d))
            for d in (2, 1, 3)
        ])

    def group_total(h):
        total = rc[h, 0].astype(F32)
        for s in range(1, 4):
            total = total + rc[h, s].astype(F32)
        group = total.astype(BF16)
        tsum[h] = group
        recvy[h, row_at] = group
        return start([
            copy(tsum.at[h], recvy.at[h, row_at], sy.at[h, d - 1], ry.at[h, d - 1], at_row(d))
            for d in (4, 3, 5, 2, 6, 1, 7)
        ])

    def row_total(h):
        total = recvy[h, 0].astype(F32)
        for s in range(1, 8):
            total = total + recvy[h, s].astype(F32)
        row = total.astype(BF16)
        rbuf[h] = row
        recvx[h, x] = row
        return start([
            copy(rbuf.at[h], recvx.at[h, x], sx.at[h, d - 1], rx.at[h, d - 1], at_x(d))
            for d in (2, 1, 3)
        ])

    def earlier_groups(h):
        state = jnp.where(row_at > 0, recvy[h, 0].astype(F32), 0.0)
        for s in range(1, 7):
            state = state + jnp.where(s < row_at, recvy[h, s].astype(F32), 0.0)
        for s in range(3):
            state = state + jnp.where(s < x, recvx[h, s].astype(F32), 0.0)
        for s in range(4):
            sendc[h, s] = state.astype(BF16)
            if s < 3:
                state = state + rc[h, s].astype(F32)
        enter[h, a] = sendc[h, a]
        return start([
            copy(sendc.at[h, step(a, d)], enter.at[h, a],
                 sc2.at[h, d - 1], qc2.at[h, d - 1], at_a(d))
            for d in (2, 1, 3)
        ])

    def back_to_pairs(h):
        for i in range(4):
            state = enter[h, i].astype(F32)
            first = psum[h, 4 * p + i].astype(F32)
            sendb[h, i] = (state + jnp.where(p == 0, first, 0.0)).astype(BF16)
            second = rb[h, i].astype(F32)
            pair_enter[h, 4 * p + i] = (state + jnp.where(p == 1, second, 0.0)).astype(BF16)
        return start([
            copy(sendb.at[h], pair_enter.at[h, pl.ds(4 * p, 4)], sb2.at[h], qb2.at[h], at_p)
        ])

    def back_to_blocks(h):
        for i in range(8):
            head = 16 * h + 8 * e + i
            state = pair_enter[h, i].astype(F32)
            first = own[head].astype(F32)
            senda[h, i] = (state + jnp.where(e == 0, first, 0.0)).astype(BF16)
            second = ra[h, i].astype(F32)
            fin[head] = (state + jnp.where(e == 1, second, 0.0)).astype(BF16)
        return start([
            copy(senda.at[h], fin.at[pl.ds(16 * h + 8 * e, 8)], sa2.at[h], qa2.at[h], at_e)
        ])

    steps = [
        (pair_total, 4.5), (cluster_total, 10.0), (group_total, 19.0), (row_total, 22.5),
        (earlier_groups, 26.0), (back_to_pairs, 35.0), (back_to_blocks, 40.5),
        (outer_products, 45.5),
    ]
    order = sorted(
        (when + 4.0 * h, h, n) for n, (_, when) in enumerate(steps) for h in range(PIECES)
    )
    flying = {0: to_pairs(0)}
    own_states(1)
    flying[1] = to_pairs(1)
    own_states(2)
    own_states(3)
    loads[-1].wait()
    for _, h, n in order:
        arrive(flying[h])
        flying[h] = steps[n][0](h)
        if n == 0:
            if h + 2 < PIECES:
                flying[h + 2] = to_pairs(h + 2)
            inner_products(h)
    for one in started:
        one.wait_send()
    for h in range(PIECES):
        flying[h].wait()


def norm_kernel(attended, gain, out):
    wide = attended[...].astype(F32)
    meansq = jnp.mean(wide * wide, axis=1, keepdims=True)
    out[...] = (wide * lax.rsqrt(meansq + 1e-06) * gain[...]).astype(BF16)


def per_device(queries, keys, values, gain):
    rows, feat = queries.shape

    def buf(*lead):
        return pltpu.VMEM((*lead, ROWS, E), BF16)

    dma = pltpu.SemaphoreType.DMA
    n = PIECES
    one = [dma((n,)), dma((n,))]
    three = [dma((n, 3)), dma((n, 3))]
    seven = [dma((n, 7)), dma((n, 7))]
    hbm = pl.BlockSpec(memory_space=pltpu.HBM)
    tokens = pltpu.VMEM((rows, feat), BF16)
    attended = pl.pallas_call(
        attention_kernel,
        out_shape=jax.ShapeDtypeStruct((rows, feat), BF16),
        in_specs=[hbm, hbm, hbm],
        out_specs=hbm,
        scratch_shapes=[
            tokens, tokens, tokens, pltpu.VMEM((rows, feat), F32), tokens,
            buf(2 * HEADS), dma((2 * PIECES + 1,)), dma((n,)),
            buf(n, 8), buf(n, 8), buf(n, 4), buf(n, 4), buf(n, 4),
            buf(n), buf(n, 8), buf(n), buf(n, 4),
            buf(n, 4), buf(n, 4), buf(n, 4), buf(n, 8), buf(n, 8), buf(2 * HEADS),
            *one, *one, *three, *seven, *three, *three, *one, *one,
        ],
        compiler_params=pltpu.CompilerParams(
            collective_id=0, has_side_effects=True, vmem_limit_bytes=65600000
        ),
    )(queries, keys, values)
    return pl.pallas_call(
        norm_kernel,
        out_shape=jax.ShapeDtypeStruct((rows, feat), BF16),
        grid=(4,),
        in_specs=[
            pl.BlockSpec((rows // 4, feat), lambda i: (i, 0)),
            pl.BlockSpec((1, feat), lambda i: (0, 0)),
        ],
        out_specs=pl.BlockSpec((rows // 4, feat), lambda i: (i, 0)),
    )(attended, gain.reshape(1, feat))


def solution(mesh):
    return jax.shard_map(
        per_device,
        mesh=mesh,
        in_specs=(
            P(("seq", "head"), None),
            P(("seq", "head"), None),
            P(("seq", "head"), None),
            P(),
        ),
        out_specs=P(("seq", "head"), None),
        check_vma=False,
    )
```

```python
import jax
import jax.numpy as jnp
from jax import lax
from jax.experimental import pallas as pl
from jax.experimental.pallas import tpu as pltpu
from jax.sharding import PartitionSpec as P

E = 128
HEADS = 32
PIECES = 4
ROWS = 64
AHEAD = 2
APART = 4.0
F32 = jnp.float32
BF16 = jnp.bfloat16
MESH = pl.DeviceIdType.MESH


def attention_kernel(
    q_hbm, k_hbm, v_hbm, gain, out,
    q, k, v, inner, squares, own, load,
    ra, psum, rb, ctot, rc, tsum, recvy, rbuf, recvx,
    sendc, enter, sendb, pair_enter, senda, fin,
    sa, qa, sb, qb, sc, qc, sy, ry, sx, rx, sc2, qc2, sb2, qb2, sa2, qa2,
):
    g = lax.axis_index("seq")
    z = lax.axis_index("head")
    a, b = lax.div(z, 4), lax.rem(z, 4)
    p, e = lax.div(b, 2), lax.rem(b, 2)
    x = lax.div(g, 8)

    def step(v, d):
        return lax.rem(v + d, 4)

    at_e = {"seq": g, "head": z + 1 - 2 * e}
    at_p = {"seq": g, "head": z + 2 - 4 * p}

    def at_a(d):
        return {"seq": g, "head": step(a, d) * 4 + b}

    row_at = lax.rem(g, 8)

    def at_row(d):
        return {"seq": x * 8 + lax.rem(row_at + d, 8), "head": z}

    def at_x(d):
        return {"seq": step(x, d) * 8 + row_at, "head": z}

    def copy(src, dst, send, recv, where):
        return pltpu.make_async_remote_copy(
            src_ref=src, dst_ref=dst, send_sem=send, recv_sem=recv,
            device_id=where, device_id_type=MESH,
        )

    started = []

    def start(copies):
        for one in copies:
            one.start()
        started.extend(copies)
        return copies

    def arrive(copies):
        for one in copies:
            one.wait_recv()

    barrier = pltpu.get_barrier_semaphore()
    peers = [f(d) for f in (at_a, at_x) for d in (1, 2, 3)]
    peers.extend([at_e, at_p])
    peers.extend(at_row(d) for d in range(1, 8))
    for peer in peers:
        pl.semaphore_signal(barrier, inc=1, device_id=peer, device_id_type=MESH)

    wide = 8 * E
    loads = [
        pltpu.make_async_copy(
            src.at[:, pl.ds(h * wide, wide)], dst.at[:, pl.ds(h * wide, wide)], load.at[2 * h + i]
        )
        for h in range(PIECES)
        for i, (src, dst) in enumerate(((k_hbm, k), (v_hbm, v)))
    ]
    loads.append(pltpu.make_async_copy(q_hbm, q, load.at[2 * PIECES]))
    for one in loads:
        one.start()

    def cols(head):
        return pl.ds(pl.multiple_of(head * E, E), E)

    def own_states(h):
        loads[2 * h].wait()
        loads[2 * h + 1].wait()
        for head in range(8 * h, 8 * h + 8):
            at = pl.ds(head * E, E)
            state = lax.dot_general(
                k[:, at], v[:, at], (((0,), (0,)), ((), ())), preferred_element_type=F32
            )
            own[pl.ds(2 * head, 2)] = state.astype(BF16).reshape(2, ROWS, E)

    def inner_products(h):
        lower = lax.broadcasted_iota(jnp.int32, (E, E), 0) >= lax.broadcasted_iota(
            jnp.int32, (E, E), 1
        )

        def body(j, carry):
            for i in range(4):
                at = cols(8 * h + 4 * j + i)
                scores = lax.dot_general(
                    q[:, at], k[:, at], (((1,), (1,)), ((), ())), preferred_element_type=F32
                )
                scores = jnp.where(lower, scores, 0.0).astype(BF16)
                inner[:, at] = jnp.dot(scores, v[:, at], preferred_element_type=F32)
            return carry

        lax.fori_loop(0, 2, body, 0)

    def outer_products(h):
        def body(j, carry):
            total = squares[...]
            for i in range(4):
                head = 8 * h + 4 * j + i
                at = cols(head)
                state = fin[pl.ds(2 * head, 2)].reshape(E, E)
                outer = jnp.dot(q[:, at], state, preferred_element_type=F32)
                attended = (inner[:, at] + outer).astype(BF16)
                out[:, at] = attended
                wide = attended.astype(F32)
                total = total + wide * wide
            squares[...] = total
            return carry

        lax.fori_loop(0, 2, body, 0)

    own_states(0)
    pl.semaphore_wait(barrier, len(peers))

    def to_pairs(h):
        return start([copy(own.at[pl.ds(16 * h + 8 * (1 - e), 8)], ra.at[h], sa.at[h], qa.at[h], at_e)])

    def pair_total(h):
        for i in range(8):
            mine = own[16 * h + 8 * e + i].astype(F32)
            psum[h, i] = (mine + ra[h, i].astype(F32)).astype(BF16)
        return start([copy(psum.at[h, pl.ds(4 * (1 - p), 4)], rb.at[h], sb.at[h], qb.at[h], at_p)])

    def cluster_total(h):
        for i in range(4):
            total = psum[h, 4 * p + i].astype(F32) + rb[h, i].astype(F32)
            ctot[h, i] = total.astype(BF16)
        rc[h, a] = ctot[h, a]
        return start([
            copy(ctot.at[h, step(a, d)], rc.at[h, a],
                 sc.at[h, d - 1], qc.at[h, d - 1], at_a(d))
            for d in (2, 1, 3)
        ])

    def group_total(h):
        total = rc[h, 0].astype(F32)
        for s in range(1, 4):
            total = total + rc[h, s].astype(F32)
        group = total.astype(BF16)
        tsum[h] = group
        recvy[h, row_at] = group
        return start([
            copy(tsum.at[h], recvy.at[h, row_at], sy.at[h, d - 1], ry.at[h, d - 1], at_row(d))
            for d in (4, 3, 5, 2, 6, 1, 7)
        ])

    def row_total(h):
        total = recvy[h, 0].astype(F32)
        for s in range(1, 8):
            total = total + recvy[h, s].astype(F32)
        row = total.astype(BF16)
        rbuf[h] = row
        recvx[h, x] = row
        return start([
            copy(rbuf.at[h], recvx.at[h, x], sx.at[h, d - 1], rx.at[h, d - 1], at_x(d))
            for d in (2, 1, 3)
        ])

    def earlier_groups(h):
        state = jnp.where(row_at > 0, recvy[h, 0].astype(F32), 0.0)
        for s in range(1, 7):
            state = state + jnp.where(s < row_at, recvy[h, s].astype(F32), 0.0)
        for s in range(3):
            state = state + jnp.where(s < x, recvx[h, s].astype(F32), 0.0)
        for s in range(4):
            sendc[h, s] = state.astype(BF16)
            if s < 3:
                state = state + rc[h, s].astype(F32)
        enter[h, a] = sendc[h, a]
        return start([
            copy(sendc.at[h, step(a, d)], enter.at[h, a],
                 sc2.at[h, d - 1], qc2.at[h, d - 1], at_a(d))
            for d in (2, 1, 3)
        ])

    def back_to_pairs(h):
        for i in range(4):
            state = enter[h, i].astype(F32)
            first = psum[h, 4 * p + i].astype(F32)
            sendb[h, i] = (state + jnp.where(p == 0, first, 0.0)).astype(BF16)
            second = rb[h, i].astype(F32)
            pair_enter[h, 4 * p + i] = (state + jnp.where(p == 1, second, 0.0)).astype(BF16)
        return start([
            copy(sendb.at[h], pair_enter.at[h, pl.ds(4 * p, 4)], sb2.at[h], qb2.at[h], at_p)
        ])

    def back_to_blocks(h):
        for i in range(8):
            head = 16 * h + 8 * e + i
            state = pair_enter[h, i].astype(F32)
            first = own[head].astype(F32)
            senda[h, i] = (state + jnp.where(e == 0, first, 0.0)).astype(BF16)
            second = ra[h, i].astype(F32)
            fin[head] = (state + jnp.where(e == 1, second, 0.0)).astype(BF16)
        return start([
            copy(senda.at[h], fin.at[pl.ds(16 * h + 8 * e, 8)], sa2.at[h], qa2.at[h], at_e)
        ])

    steps = [
        (pair_total, 4.5), (cluster_total, 10.0), (group_total, 19.0), (row_total, 22.5),
        (earlier_groups, 26.0), (back_to_pairs, 35.0), (back_to_blocks, 40.5),
        (outer_products, 45.5),
    ]
    order = sorted(
        (when + APART * h, h, n) for n, (_, when) in enumerate(steps) for h in range(PIECES)
    )
    flying = {0: to_pairs(0)}
    for h in range(1, PIECES):
        own_states(h)
        if h < AHEAD:
            flying[h] = to_pairs(h)
    squares[...] = jnp.zeros_like(squares)
    loads[-1].wait()
    for _, h, n in order:
        arrive(flying[h])
        flying[h] = steps[n][0](h)
        if n == 0:
            if h + AHEAD < PIECES:
                flying[h + AHEAD] = to_pairs(h + AHEAD)
            inner_products(h)
    meansq = jnp.sum(squares[...], axis=1, keepdims=True) * (1.0 / (HEADS * E))
    scale = lax.rsqrt(meansq + 1e-06)

    def norm(j, carry):
        for i in range(4):
            at = cols(4 * j + i)
            out[:, at] = (out[:, at].astype(F32) * scale * gain[:, at]).astype(BF16)
        return carry

    lax.fori_loop(0, HEADS // 4, norm, 0)
    for one in started:
        one.wait_send()


def per_device(queries, keys, values, gain):
    rows, feat = queries.shape

    def buf(*lead):
        return pltpu.VMEM((*lead, ROWS, E), BF16)

    dma = pltpu.SemaphoreType.DMA
    n = PIECES
    one = [dma((n,)), dma((n,))]
    three = [dma((n, 3)), dma((n, 3))]
    seven = [dma((n, 7)), dma((n, 7))]
    hbm = pl.BlockSpec(memory_space=pltpu.HBM)
    vmem = pl.BlockSpec(memory_space=pltpu.VMEM)
    tokens = pltpu.VMEM((rows, feat), BF16)
    return pl.pallas_call(
        attention_kernel,
        out_shape=jax.ShapeDtypeStruct((rows, feat), BF16),
        in_specs=[hbm, hbm, hbm, vmem],
        out_specs=vmem,
        scratch_shapes=[
            tokens, tokens, tokens, pltpu.VMEM((rows, feat), F32), pltpu.VMEM((rows, E), F32),
            buf(2 * HEADS), dma((2 * PIECES + 1,)),
            buf(n, 8), buf(n, 8), buf(n, 4), buf(n, 4), buf(n, 4),
            buf(n), buf(n, 8), buf(n), buf(n, 4),
            buf(n, 4), buf(n, 4), buf(n, 4), buf(n, 8), buf(n, 8), buf(2 * HEADS),
            *one, *one, *three, *seven, *three, *three, *one, *one,
        ],
        compiler_params=pltpu.CompilerParams(
            collective_id=0, has_side_effects=True, vmem_limit_bytes=65600000
        ),
    )(queries, keys, values, gain.reshape(1, feat))


def solution(mesh):
    return jax.shard_map(
        per_device,
        mesh=mesh,
        in_specs=(
            P(("seq", "head"), None),
            P(("seq", "head"), None),
            P(("seq", "head"), None),
            P(),
        ),
        out_specs=P(("seq", "head"), None),
        check_vma=False,
    )
```

```python
import jax
import jax.numpy as jnp
from jax import lax
from jax.experimental import pallas as pl
from jax.experimental.pallas import tpu as pltpu
from jax.sharding import PartitionSpec as P

E = 128
HEADS = 32
PIECES = 4
ROWS = 64
AHEAD = 3
APART = 4.0
F32 = jnp.float32
BF16 = jnp.bfloat16
MESH = pl.DeviceIdType.MESH


def attention_kernel(
    q_hbm, k_hbm, v_hbm, gain, out,
    q, k, v, inner, squares, own, load,
    ra, psum, rb, ctot, rc, tsum, recvy, rbuf, recvx,
    sendc, enter, sendb, pair_enter, senda, fin,
    sa, qa, sb, qb, sc, qc, sy, ry, sx, rx, sc2, qc2, sb2, qb2, sa2, qa2,
):
    g = lax.axis_index("seq")
    z = lax.axis_index("head")
    a, b = lax.div(z, 4), lax.rem(z, 4)
    p, e = lax.div(b, 2), lax.rem(b, 2)
    x = lax.div(g, 8)

    def step(v, d):
        return lax.rem(v + d, 4)

    at_e = {"seq": g, "head": z + 1 - 2 * e}
    at_p = {"seq": g, "head": z + 2 - 4 * p}

    def at_a(d):
        return {"seq": g, "head": step(a, d) * 4 + b}

    row_at = lax.rem(g, 8)

    def at_row(d):
        return {"seq": x * 8 + lax.rem(row_at + d, 8), "head": z}

    def at_x(d):
        return {"seq": step(x, d) * 8 + row_at, "head": z}

    def copy(src, dst, send, recv, where):
        return pltpu.make_async_remote_copy(
            src_ref=src, dst_ref=dst, send_sem=send, recv_sem=recv,
            device_id=where, device_id_type=MESH,
        )

    started = []

    def start(copies):
        for one in copies:
            one.start()
        started.extend(copies)
        return copies

    def arrive(copies):
        for one in copies:
            one.wait_recv()

    barrier = pltpu.get_barrier_semaphore()
    peers = [f(d) for f in (at_a, at_x) for d in (1, 2, 3)]
    peers.extend([at_e, at_p])
    peers.extend(at_row(d) for d in range(1, 8))
    for peer in peers:
        pl.semaphore_signal(barrier, inc=1, device_id=peer, device_id_type=MESH)

    wide = 8 * E
    loads = [
        pltpu.make_async_copy(
            src.at[:, pl.ds(h * wide, wide)], dst.at[:, pl.ds(h * wide, wide)], load.at[2 * h + i]
        )
        for h in range(PIECES)
        for i, (src, dst) in enumerate(((k_hbm, k), (v_hbm, v)))
    ]
    loads.append(pltpu.make_async_copy(q_hbm, q, load.at[2 * PIECES]))
    for one in loads:
        one.start()

    def cols(head):
        return pl.ds(pl.multiple_of(head * E, E), E)

    def own_states(h):
        loads[2 * h].wait()
        loads[2 * h + 1].wait()
        for head in range(8 * h, 8 * h + 8):
            at = pl.ds(head * E, E)
            state = lax.dot_general(
                k[:, at], v[:, at], (((0,), (0,)), ((), ())), preferred_element_type=F32
            )
            own[pl.ds(2 * head, 2)] = state.astype(BF16).reshape(2, ROWS, E)

    def inner_products(h):
        lower = lax.broadcasted_iota(jnp.int32, (E, E), 0) >= lax.broadcasted_iota(
            jnp.int32, (E, E), 1
        )

        def body(j, carry):
            for i in range(4):
                at = cols(8 * h + 4 * j + i)
                scores = lax.dot_general(
                    q[:, at], k[:, at], (((1,), (1,)), ((), ())), preferred_element_type=F32
                )
                scores = jnp.where(lower, scores, 0.0).astype(BF16)
                inner[:, at] = jnp.dot(scores, v[:, at], preferred_element_type=F32)
            return carry

        lax.fori_loop(0, 2, body, 0)

    def outer_products(h):
        def body(j, carry):
            total = squares[...]
            for i in range(4):
                head = 8 * h + 4 * j + i
                at = cols(head)
                state = fin[pl.ds(2 * head, 2)].reshape(E, E)
                outer = jnp.dot(q[:, at], state, preferred_element_type=F32)
                attended = (inner[:, at] + outer).astype(BF16)
                out[:, at] = attended
                wide = attended.astype(F32)
                total = total + wide * wide
            squares[...] = total
            return carry

        lax.fori_loop(0, 2, body, 0)

    own_states(0)
    pl.semaphore_wait(barrier, len(peers))

    def to_pairs(h):
        return start([copy(own.at[pl.ds(16 * h + 8 * (1 - e), 8)], ra.at[h], sa.at[h], qa.at[h], at_e)])

    def pair_total(h):
        for i in range(8):
            mine = own[16 * h + 8 * e + i].astype(F32)
            psum[h, i] = (mine + ra[h, i].astype(F32)).astype(BF16)
        return start([copy(psum.at[h, pl.ds(4 * (1 - p), 4)], rb.at[h], sb.at[h], qb.at[h], at_p)])

    def cluster_total(h):
        for i in range(4):
            total = psum[h, 4 * p + i].astype(F32) + rb[h, i].astype(F32)
            ctot[h, i] = total.astype(BF16)
        rc[h, a] = ctot[h, a]
        return start([
            copy(ctot.at[h, step(a, d)], rc.at[h, a],
                 sc.at[h, d - 1], qc.at[h, d - 1], at_a(d))
            for d in (2, 1, 3)
        ])

    def group_total(h):
        total = rc[h, 0].astype(F32)
        for s in range(1, 4):
            total = total + rc[h, s].astype(F32)
        group = total.astype(BF16)
        tsum[h] = group
        recvy[h, row_at] = group
        return start([
            copy(tsum.at[h], recvy.at[h, row_at], sy.at[h, d - 1], ry.at[h, d - 1], at_row(d))
            for d in (4, 3, 5, 2, 6, 1, 7)
        ])

    def row_total(h):
        total = recvy[h, 0].astype(F32)
        for s in range(1, 8):
            total = total + recvy[h, s].astype(F32)
        row = total.astype(BF16)
        rbuf[h] = row
        recvx[h, x] = row
        return start([
            copy(rbuf.at[h], recvx.at[h, x], sx.at[h, d - 1], rx.at[h, d - 1], at_x(d))
            for d in (2, 1, 3)
        ])

    def earlier_groups(h):
        state = jnp.where(row_at > 0, recvy[h, 0].astype(F32), 0.0)
        for s in range(1, 7):
            state = state + jnp.where(s < row_at, recvy[h, s].astype(F32), 0.0)
        for s in range(3):
            state = state + jnp.where(s < x, recvx[h, s].astype(F32), 0.0)
        for s in range(4):
            sendc[h, s] = state.astype(BF16)
            if s < 3:
                state = state + rc[h, s].astype(F32)
        enter[h, a] = sendc[h, a]
        return start([
            copy(sendc.at[h, step(a, d)], enter.at[h, a],
                 sc2.at[h, d - 1], qc2.at[h, d - 1], at_a(d))
            for d in (2, 1, 3)
        ])

    def back_to_pairs(h):
        for i in range(4):
            state = enter[h, i].astype(F32)
            first = psum[h, 4 * p + i].astype(F32)
            sendb[h, i] = (state + jnp.where(p == 0, first, 0.0)).astype(BF16)
            second = rb[h, i].astype(F32)
            pair_enter[h, 4 * p + i] = (state + jnp.where(p == 1, second, 0.0)).astype(BF16)
        return start([
            copy(sendb.at[h], pair_enter.at[h, pl.ds(4 * p, 4)], sb2.at[h], qb2.at[h], at_p)
        ])

    def back_to_blocks(h):
        for i in range(8):
            head = 16 * h + 8 * e + i
            state = pair_enter[h, i].astype(F32)
            first = own[head].astype(F32)
            senda[h, i] = (state + jnp.where(e == 0, first, 0.0)).astype(BF16)
            second = ra[h, i].astype(F32)
            fin[head] = (state + jnp.where(e == 1, second, 0.0)).astype(BF16)
        return start([
            copy(senda.at[h], fin.at[pl.ds(16 * h + 8 * e, 8)], sa2.at[h], qa2.at[h], at_e)
        ])

    steps = [
        (pair_total, 4.5), (cluster_total, 10.0), (group_total, 19.0), (row_total, 22.5),
        (earlier_groups, 26.0), (back_to_pairs, 35.0), (back_to_blocks, 40.5),
        (outer_products, 45.5),
    ]
    order = sorted(
        (when + APART * h, h, n) for n, (_, when) in enumerate(steps) for h in range(PIECES)
    )
    flying = {0: to_pairs(0)}
    for h in range(1, PIECES):
        own_states(h)
        if h < AHEAD:
            flying[h] = to_pairs(h)
    squares[...] = jnp.zeros_like(squares)
    loads[-1].wait()
    for _, h, n in order:
        arrive(flying[h])
        flying[h] = steps[n][0](h)
        if n == 0:
            if h + AHEAD < PIECES:
                flying[h + AHEAD] = to_pairs(h + AHEAD)
            inner_products(h)
    meansq = jnp.sum(squares[...], axis=1, keepdims=True) * (1.0 / (HEADS * E))
    scale = lax.rsqrt(meansq + 1e-06)

    def norm(j, carry):
        for i in range(4):
            at = cols(4 * j + i)
            out[:, at] = (out[:, at].astype(F32) * scale * gain[:, at]).astype(BF16)
        return carry

    lax.fori_loop(0, HEADS // 4, norm, 0)
    for one in started:
        one.wait_send()


def per_device(queries, keys, values, gain):
    rows, feat = queries.shape

    def buf(*lead):
        return pltpu.VMEM((*lead, ROWS, E), BF16)

    dma = pltpu.SemaphoreType.DMA
    n = PIECES
    one = [dma((n,)), dma((n,))]
    three = [dma((n, 3)), dma((n, 3))]
    seven = [dma((n, 7)), dma((n, 7))]
    hbm = pl.BlockSpec(memory_space=pltpu.HBM)
    vmem = pl.BlockSpec(memory_space=pltpu.VMEM)
    tokens = pltpu.VMEM((rows, feat), BF16)
    return pl.pallas_call(
        attention_kernel,
        out_shape=jax.ShapeDtypeStruct((rows, feat), BF16),
        in_specs=[hbm, hbm, hbm, vmem],
        out_specs=vmem,
        scratch_shapes=[
            tokens, tokens, tokens, pltpu.VMEM((rows, feat), F32), pltpu.VMEM((rows, E), F32),
            buf(2 * HEADS), dma((2 * PIECES + 1,)),
            buf(n, 8), buf(n, 8), buf(n, 4), buf(n, 4), buf(n, 4),
            buf(n), buf(n, 8), buf(n), buf(n, 4),
            buf(n, 4), buf(n, 4), buf(n, 4), buf(n, 8), buf(n, 8), buf(2 * HEADS),
            *one, *one, *three, *seven, *three, *three, *one, *one,
        ],
        compiler_params=pltpu.CompilerParams(
            collective_id=0, has_side_effects=True, vmem_limit_bytes=65600000
        ),
    )(queries, keys, values, gain.reshape(1, feat))


def solution(mesh):
    return jax.shard_map(
        per_device,
        mesh=mesh,
        in_specs=(
            P(("seq", "head"), None),
            P(("seq", "head"), None),
            P(("seq", "head"), None),
            P(),
        ),
        out_specs=P(("seq", "head"), None),
        check_vma=False,
    )
```
